128 devices in a mesh: shard: 32 (over y, x, core), grp: 4 (over z).
Axes of the slice: x: 4, y: 4, z: 4, core: 2. Of those that a mesh axis runs over, the one named last changes fastest.
Arguments:
- embeddings: float32 [65536, 1024], P(('shard', 'grp')), may hold values from -6 to 6
- cluster: int32 [65536, 1], P(('shard', 'grp')), may hold values from 0 to 31; in each aligned block of 512 rows (0 to 511, 512 to 1023, ...) at most 32 rows name the same one
Outputs:
- duplicate: float32 [65536], P(('shard', 'grp'))
- neighbour: float32 [65536, 1024], P(('shard', 'grp'))
The draws below stay inside these ranges and needn't reach their ends.
Inputs may be any that keep to these rules, and one draw needn't show every extreme that they name: Among the pages of one device, at most 32 belong to any one cluster.
All inputs are finite; a program needn't handle non-finite values.
Results may differ from the reference program's by a relative error of at most 0.0075.
Values may be sent and summed in bfloat16 or wider, within the bound.
A program may use at most 128 MiB of HBM per device.

```python
import math
import jax
import jax.numpy as jnp
import numpy as np
from jax import lax

D = 1024
PAGES_DEV = 512
SLOT = 32
NCL = 32
CAP = 4096
PAGES = 65536


def levels(key, extent, cuts, least, top_value):
    def one(axis_at, blocks):
        steps = jax.random.uniform(jax.random.fold_in(jax.random.fold_in(key, 6), axis_at), (blocks,), jnp.float32, least / len(cuts), top_value / len(cuts))
        return jnp.repeat(jnp.exp(steps), extent[axis_at] // blocks).reshape((-1,) + (1,) * (len(extent) - axis_at - 1))

    factor_of = one(*cuts[0])
    for cut in cuts[1:]:
        factor_of = factor_of * one(*cut)
    return factor_of


def routed_block(rng, own, number, rows, count, top, limit, slope):
    sequence = jax.random.permutation(rng, count)
    heavy_load, usual = load_shares(count, rows * top, limit, slope, True), load_shares(count, rows * top, limit, slope, False)
    places = jnp.arange(count)

    def named(lengths, offset_by):
        used = int((lengths > 0).sum())
        fixed = max(1, used // 4)
        moved = fixed + (places - fixed + offset_by * (used - fixed)) % max(1, count - fixed)
        return jnp.zeros((count,), jnp.int32).at[sequence[jnp.where(places < fixed, places, moved)]].set(jnp.asarray(lengths, jnp.int32))

    lengths = jnp.where(number % 4 == 0, named(heavy_load, number // 4), named(usual, number - number // 4 - 1))
    mixed = jax.random.permutation(jax.random.fold_in(own, 3), count)
    donor, sink = mixed[0:count // 2 * 2:2], mixed[1:count // 2 * 2:2]
    room = jnp.minimum(lengths[donor] - 1, limit - lengths[sink]) // 2
    room = jnp.where((donor == sequence[0]) | (sink == sequence[0]) | (lengths[sink] == 0), 0, jnp.maximum(room, 0))
    moved = jax.random.randint(jax.random.fold_in(own, 4), (count // 2,), 0, 1 << 20) % (room + 1)
    lengths = lengths.at[donor].add(-moved).at[sink].add(moved)
    labels = jnp.searchsorted(jnp.cumsum(lengths), jnp.arange(rows * top), side="right").astype(jnp.int32)
    listing = labels.reshape(top, rows).T
    listing = listing[jax.random.permutation(jax.random.fold_in(own, 1), rows)]
    offset_by = jax.random.randint(jax.random.fold_in(own, 2), (rows, 1), 0, top)
    return jnp.take_along_axis(listing, (jnp.arange(top)[None, :] + offset_by) % top, axis=1)


def load_shares(number_of, total, reach, slope, full):
    portions = [(1 << 20) // math.isqrt(grade ** slope) + 1 for grade in range(1, number_of + 1)]
    largest = reach if full else min(reach, max(-(-total // number_of), total * portions[0] // sum(portions)))
    least = 1 if total - largest >= number_of - 1 else 0
    given, spare = [largest] + [least] * (number_of - 1), total - largest - least * (number_of - 1)
    while spare > 0:
        free = [i for i in range(1, number_of) if given[i] < largest] or [i for i in range(1, number_of) if given[i] < reach]
        mass, remaining = sum([portions[i] for i in free]), spare
        for i in free:
            extra = min(reach - given[i], max(1, remaining * portions[i] // mass), spare)
            given[i] = given[i] + extra
            spare = spare - extra
    return np.array(given)


def noise(rng, extent, scale, bound, shards=(), held_as=jnp.bfloat16):
    entries = scale * jax.random.normal(rng, extent, jnp.float32)
    if shards:
        entries = entries * levels(rng, extent, shards, -0.22, 0.18)
    return jnp.clip(entries, -bound, bound).astype(held_as)


def setup_inputs(seed: int = 0) -> dict:
    streams_of = jax.random.split(jax.random.key(seed), 3)
    embeddings = noise(streams_of[0], (PAGES, D), 1.0, 6.0, ((0, 128),), jnp.float32)
    cluster_keys = jax.random.split(jax.random.fold_in(streams_of[1], 1), PAGES // PAGES_DEV)
    cluster_turns = jax.random.permutation(jax.random.fold_in(streams_of[1], 3), PAGES // PAGES_DEV)
    cluster = jax.vmap(lambda own, number: routed_block(jax.random.fold_in(streams_of[1], 2), own, number, PAGES_DEV, NCL, 1, SLOT, 2))(cluster_keys, cluster_turns).reshape((PAGES, 1))
    return dict(embeddings=embeddings, cluster=cluster)


def normalize(embeddings):
    scale = lax.rsqrt(lax.optimization_barrier(jnp.mean(embeddings * embeddings, axis=1, keepdims=True)) + 1e-06)
    return (embeddings * scale).astype(jnp.bfloat16)

def reference(embeddings, cluster):
    npages = embeddings.shape[0]
    width = embeddings.shape[1]
    units = normalize(embeddings)
    ids = cluster[:, 0].astype(jnp.int32)
    onehot = (ids[:, None] == jnp.arange(NCL, dtype=jnp.int32)[None, :]).astype(jnp.int32)
    rank = (lax.optimization_barrier(jnp.sum(jnp.cumsum(onehot, axis=0) * onehot, axis=1)) - 1).astype(jnp.int32)
    members = jnp.zeros((NCL, CAP), jnp.int32).at[ids, rank].set(jnp.arange(npages, dtype=jnp.int32))
    live = jnp.zeros((NCL, CAP), jnp.float32).at[ids, rank].set(1.0)
    others = 1.0 - jnp.eye(CAP, dtype=jnp.float32)

    def per_cluster(packed):
        index, valid = packed
        rows = units[index]
        scores = jnp.dot(rows, rows.T, preferred_element_type=jnp.float32) * (64.0 / width)
        weight = jnp.exp(scores) * valid[None, :] * others
        count = lax.optimization_barrier(jnp.sum(weight, axis=1))
        pull = jnp.dot(weight.astype(jnp.bfloat16), rows, preferred_element_type=jnp.float32)
        return (jnp.log1p(count), pull / (1.0 + count)[:, None])
    dups, pulls = lax.map(per_cluster, (members, live))
    return (dups[ids, rank], pulls[ids, rank])
```

```python
import functools
import math

import jax
import jax.numpy as jnp
from jax import lax
from jax.experimental import pallas as pl
from jax.experimental.pallas import tpu as pltpu
from jax.sharding import PartitionSpec as P

SLOT = 32
LANES = 128
BF = jnp.bfloat16
F32 = jnp.float32
OWN, CROSS, PARTNER, FAR = range(4)


def kernel(
    ny, nx, nz,
    emb, idr, idc, near, dup,
    ob, f0, xs, fx, rl, fr, acc, cn, res, dsend, back, drecv, unpack, lane_of,
    s1s, s1r, rls, rlr, xrs, xrr, pws, pwr, pfs, pfr, sbs, sbr,
    fos, fors, frs, frr, fbs, fbr, res_s, res_r, dus, dur,
):
    ncol = ny * nx
    ncl = 2 * ncol
    pages, width = emb.shape
    brow = ncol * SLOT
    shard, z = lax.axis_index("shard"), lax.axis_index("grp")
    q, core = shard // 2, shard % 2
    y, x = q // nx, q % nx
    partner_z = z + 1 - 2 * (z % 2)
    cross_z = nz - 1 - z
    side = z // 2

    def column(i, sign):
        dy, dx = i // nx, i % nx
        yy = lax.rem(y + (dy if sign > 0 else ny - dy), ny)
        xx = lax.rem(x + (dx if sign > 0 else nx - dx), nx)
        return yy * nx + xx

    def at(col, c, zz):
        return {"shard": col * 2 + c, "grp": zz}

    def far(i):
        dy, dx = i // nx, i % nx
        return min(dy, ny - dy) + min(dx, nx - dx)

    order = sorted(range(ncol), key=lambda i: (far(i), i))
    sibling = at(q, 1 - core, z)
    partner = at(q, core, partner_z)
    cross = at(q, core, cross_z)

    def rcopy(src, dst, ss, rs, dev):
        return pltpu.make_async_remote_copy(
            src_ref=src, dst_ref=dst, send_sem=ss, recv_sem=rs,
            device_id=dev, device_id_type=pl.DeviceIdType.MESH,
        )

    barrier = pltpu.get_barrier_semaphore()
    peers = [sibling, partner, cross]
    for i in range(1, ncol):
        peers.append(at(column(i, 1), core, z))
        peers.append(at(column(i, 1), core, cross_z))
    for peer in peers:
        pl.semaphore_signal(barrier, inc=1, device_id=peer, device_id_type=pl.DeviceIdType.MESH)

    def place(ids):
        col, b = ids // 2, ids % 2
        dy = lax.rem(col // nx - y + ny, ny)
        dx = lax.rem(col % nx - x + nx, nx)
        return jnp.where(b == side, 0, ncol) + dy * nx + dx

    rid_r = place(idr[...])
    hot_t = (lax.broadcasted_iota(jnp.int32, (ncl, pages), 0) == rid_r).astype(BF)
    upto = lax.broadcasted_iota(jnp.int32, (pages, pages), 0)
    upto = (upto <= lax.broadcasted_iota(jnp.int32, (pages, pages), 1)).astype(BF)
    cum_t = jnp.dot(hot_t, upto, preferred_element_type=F32)
    hot_f = hot_t.astype(F32)
    rank_r = jnp.sum(cum_t * hot_f, axis=0, keepdims=True) - 1.0
    slot_r = rid_r * SLOT + rank_r.astype(jnp.int32)
    held = jnp.sum(hot_f, axis=1, keepdims=True)
    lane = lax.broadcasted_iota(jnp.int32, (ncl, LANES), 1) % SLOT
    flags = (lane.astype(F32) < held).astype(F32)
    for c in range(ncl):
        f0[c] = flags[c : c + 1, :]

    scale = lax.rsqrt(jnp.mean(emb[...] * emb[...], axis=1, keepdims=True) + 1e-06)
    units = (emb[...] * scale).astype(BF)
    step = min(128, ncl * SLOT)
    for j in range(ncl * SLOT // step):
        pick = lax.broadcasted_iota(jnp.int32, (step, pages), 0) + j * step == slot_r
        ob[pl.ds(j * step, step), :] = jnp.dot(
            pick.astype(BF), units, preferred_element_type=F32
        ).astype(BF)

    pl.semaphore_wait(barrier, len(peers))

    def chunk(ref, i, n=1):
        return ref.at[pl.ds(i * SLOT, n * SLOT), :]

    own_in, rel_in, fo_in, fr_in, started = {}, {}, {}, {}, []
    for i in order:
        oc, rc = chunk(ob, i), chunk(ob, ncol + i)
        if i == 0:
            own_in[i] = pltpu.make_async_copy(oc, chunk(xs.at[0], 0), s1r.at[0])
            rel_in[i] = pltpu.make_async_copy(rc, chunk(rl, 0), rlr.at[0])
            fo_in[i] = pltpu.make_async_copy(f0.at[0], fx.at[0, 0], fors.at[0])
            fr_in[i] = pltpu.make_async_copy(f0.at[ncol], fr.at[0], frr.at[0])
        else:
            dev = at(column(i, 1), core, z)
            own_in[i] = rcopy(oc, chunk(xs.at[0], i), s1s.at[i], s1r.at[i], dev)
            rel_in[i] = rcopy(rc, chunk(rl, i), rls.at[i], rlr.at[i], dev)
            fo_in[i] = rcopy(f0.at[i], fx.at[0, i], fos.at[i], fors.at[i], dev)
            fr_in[i] = rcopy(f0.at[ncol + i], fr.at[i], frs.at[i], frr.at[i], dev)
            started += [own_in[i], rel_in[i], fo_in[i], fr_in[i]]
        for c in (rel_in[i], own_in[i], fo_in[i], fr_in[i]):
            c.start()

    def arrived(c, local=False):
        if local:
            c.wait()
        else:
            c.wait_recv()

    rel_out = {i: rcopy(chunk(rl, i), chunk(xs.at[2 * CROSS], i), xrs.at[i], xrr.at[i], cross) for i in range(ncol)}
    own_out = {i: rcopy(chunk(xs.at[2 * OWN], i), chunk(xs.at[2 * PARTNER], i), pws.at[i], pwr.at[i], partner) for i in range(ncol)}
    far_out = {i: rcopy(chunk(xs.at[2 * CROSS], i), chunk(xs.at[2 * FAR], i), pfs.at[i], pfr.at[i], partner) for i in range(ncol)}
    group = min(4, ncol)
    ngr = ncol // group
    sib = {
        (r, g): rcopy(
            chunk(xs.at[2 * r], order[0] if False else g * group, group),
            chunk(xs.at[2 * r + 1], g * group, group),
            sbs.at[r * ngr + g], sbr.at[r * ngr + g], sibling,
        )
        for r in range(4)
        for g in range(ngr)
    }
    flag_cross = rcopy(fr, fx.at[2 * CROSS], fbs.at[0], fbr.at[0], cross)
    flag_own = rcopy(fx.at[2 * OWN], fx.at[2 * PARTNER], fbs.at[1], fbr.at[1], partner)
    flag_far = rcopy(fx.at[2 * CROSS], fx.at[2 * FAR], fbs.at[2], fbr.at[2], partner)
    flag_sib = [rcopy(fx.at[2 * r], fx.at[2 * r + 1], fbs.at[3 + r], fbr.at[3 + r], sibling) for r in range(4)]

    def go(c):
        c.start()
        started.append(c)

    seen = {r: [0] * ngr for r in range(4)}

    def landed(r, i):
        g = i // group
        seen[r][g] += 1
        if seen[r][g] == group:
            go(sib[r, g])

    def ev_own(i):
        arrived(own_in[i], i == 0)
        go(own_out[i])
        landed(OWN, i)

    def ev_rel(i):
        arrived(rel_in[i], i == 0)
        go(rel_out[i])

    def ev_cross(i):
        arrived(rel_out[i])
        go(far_out[i])
        landed(CROSS, i)

    def ev_partner(i):
        arrived(own_out[i])
        landed(PARTNER, i)

    def ev_far(i):
        arrived(far_out[i])
        landed(FAR, i)

    def ev_flags_a():
        for i in order:
            arrived(fo_in[i], i == 0)
            arrived(fr_in[i], i == 0)
        go(flag_cross)
        go(flag_own)
        go(flag_sib[OWN])

    def ev_flags_b():
        arrived(flag_cross)
        go(flag_far)
        go(flag_sib[CROSS])
        arrived(flag_own)
        go(flag_sib[PARTNER])

    def ev_flags_c():
        arrived(flag_far)
        go(flag_sib[FAR])
        for r in range(4):
            arrived(flag_sib[r])

    def ev_unpack():
        rid_c = place(idc[...])
        hot = (lax.broadcasted_iota(jnp.int32, (pages, LANES), 1) == rid_c).astype(BF)
        below = lax.broadcasted_iota(jnp.int32, (pages, pages), 0)
        below = (below >= lax.broadcasted_iota(jnp.int32, (pages, pages), 1)).astype(BF)
        cum = jnp.dot(below, hot, preferred_element_type=F32)
        rank = (jnp.sum(cum * hot.astype(F32), axis=1, keepdims=True) - 1.0).astype(jnp.int32)
        slot = rid_c * SLOT + rank
        unpack[...] = (lax.broadcasted_iota(jnp.int32, (pages, ncl * SLOT), 1) == slot).astype(BF)
        lane_of[...] = jnp.broadcast_to((rid_c % group) * SLOT + rank, (pages, LANES))

    per = LANES // SLOT

    def mask_of(b):
        out = []
        which = lax.broadcasted_iota(jnp.int32, (1, LANES), 1) // SLOT
        for g in range(-(-ncol // per)):
            m = jnp.zeros((1, LANES), F32)
            for k in range(min(per, ncol)):
                m = jnp.where(which == k, fx[b, g * per + k], m)
            out.append(m)
        return out

    def weigh(rows, c0, r0, role, masks, diag):
        cols = xs[2 * role : 2 * role + 2].reshape(2 * brow, width)
        s = lax.dot_general(rows, cols, (((1,), (1,)), ((), ())), preferred_element_type=F32)
        w = jnp.exp2(s * (64.0 / width * math.log2(math.e)))
        if diag:
            a = lax.broadcasted_iota(jnp.int32, w.shape, 0) + r0
            w = jnp.where(a == lax.broadcasted_iota(jnp.int32, w.shape, 1), 0.0, w)
        lanes = min(LANES, brow)
        count = sum(
            w[:, k * lanes : (k + 1) * lanes] * m[:, :lanes]
            for k, m in enumerate(masks)
        )
        return count, jnp.dot(w.astype(BF), cols, preferred_element_type=F32)

    def ev_compute(rb, role):
        masks = mask_of(2 * role) + mask_of(2 * role + 1)
        count, pull = weigh(xs[2 * rb], 0, 0, role, masks, rb == role)
        sl = pl.ds(rb * brow, brow)
        if role == 0:
            cn[sl, :] = count
            acc[sl, :] = pull
        else:
            cn[sl, :] += count
            acc[sl, :] += pull

    tile = min(256, brow)

    def ev_last(t):
        masks = mask_of(2 * FAR) + mask_of(2 * FAR + 1)
        rb, r0 = t * tile // brow, t * tile % brow
        count, pull = weigh(xs[2 * rb, pl.ds(r0, tile), :], 0, r0, FAR, masks, False)
        count = cn[pl.ds(t * tile, tile), :] + count
        total = jnp.sum(count, axis=1, keepdims=True)
        pull = (acc[pl.ds(t * tile, tile), :] + pull) / (1.0 + total)
        res[pl.ds(t * tile, tile), :] = pull.astype(BF)
        value = jnp.log1p(jnp.sum(count.T, axis=0, keepdims=True))
        nl = min(LANES, brow)
        for g in range(tile // nl):
            dsend[t * (tile // nl) + g, :, pl.ds(0, nl)] = value[:, g * nl : (g + 1) * nl]
        for k in range(tile // SLOT):
            n = (t * tile) // SLOT + k
            i = n - rb * ncol
            send_back(rb, i, n)

    back_in = []

    def send_back(rb, i, n):
        dst = chunk(back, n)
        d = dsend.at[n // min(per, ncol)]
        if i == 0 and rb == 0:
            a = pltpu.make_async_copy(chunk(res, n), dst, res_r.at[n])
            b = pltpu.make_async_copy(d, drecv.at[n], dur.at[n])
            a.start()
            b.start()
        else:
            dev = at(column(i, -1), core, z if rb == 0 else cross_z)
            a = rcopy(chunk(res, n), dst, res_s.at[n], res_r.at[n], dev)
            b = rcopy(d, drecv.at[n], dus.at[n], dur.at[n], dev)
            go(a)
            go(b)
        back_in.append((a, b, i == 0 and rb == 0))

    def need_sib(r):
        for g in range(ngr):
            arrived(sib[r, g])

    events = []
    for n, i in enumerate(order):
        t = 2.0 * n
        events += [(t, ev_own, i), (t + 0.1, ev_rel, i), (t + 4, ev_cross, i)]
        events += [(2.0 + 2.6 * n, ev_partner, i), (6.0 + 3.0 * n, ev_far, i)]
    events += [(1.0, lambda _: ev_unpack(), 0)]
    events += [(30.5, lambda _: ev_flags_a(), 0), (36.5, lambda _: ev_flags_b(), 0), (37.0, lambda _: ev_flags_c(), 0)]
    first = {OWN: 37.5, CROSS: 39.5, PARTNER: 46.0}
    for r, t in first.items():
        events += [(t, need_sib, r)]
        events += [(t + 0.01, lambda a: ev_compute(*a), (0, r)), (t + 2.0, lambda a: ev_compute(*a), (1, r))]
    for _, f, a in sorted(events, key=lambda e: e[0]):
        f(a)
    need_sib(FAR)
    for t in range(2 * brow // tile):
        ev_last(t)

    for a, b, local in back_in:
        arrived(a, local)
        arrived(b, local)
    near[...] = jnp.dot(unpack[...], back[...], preferred_element_type=F32)
    got = jnp.concatenate([drecv[n] for n in range(ncl)], axis=0)
    hot = (
        lax.broadcasted_iota(jnp.int32, (pages, ncl), 1) == place(idc[...])
    ).astype(BF)
    hi = got.astype(BF)
    mid = (got - hi.astype(F32)).astype(BF)
    lo = (got - hi.astype(F32) - mid.astype(F32)).astype(BF)
    picked = sum(jnp.dot(hot, v, preferred_element_type=F32) for v in (lo, mid, hi))
    here = lax.broadcasted_iota(jnp.int32, (pages, LANES), 1) == lane_of[...]
    dup[...] = jnp.sum(jnp.where(here, picked, 0.0).T, axis=0, keepdims=True)
    for c in started:
        c.wait_send()


def local(grid, embeddings, cluster):
    pages, width = embeddings.shape
    nz = lax.axis_size("grp")
    ny, nx = grid
    ncol = ny * nx
    ncl = 2 * ncol
    brow = ncol * SLOT
    group = min(4, ncol)
    ngr = ncol // group
    dma = lambda n: pltpu.SemaphoreType.DMA((n,))
    vmem = pl.BlockSpec(memory_space=pltpu.VMEM)
    near, dup = pl.pallas_call(
        functools.partial(kernel, ny, nx, nz),
        out_shape=(
            jax.ShapeDtypeStruct((pages, width), F32),
            jax.ShapeDtypeStruct((1, pages), F32),
        ),
        in_specs=[vmem] * 3,
        out_specs=(vmem, vmem),
        scratch_shapes=[
            pltpu.VMEM((ncl * SLOT, width), BF),
            pltpu.VMEM((ncl, 1, LANES), F32),
            pltpu.VMEM((8, brow, width), BF),
            pltpu.VMEM((8, ncol, 1, LANES), F32),
            pltpu.VMEM((brow, width), BF),
            pltpu.VMEM((ncol, 1, LANES), F32),
            pltpu.VMEM((2 * brow, width), F32),
            pltpu.VMEM((2 * brow, min(LANES, brow)), F32),
            pltpu.VMEM((2 * brow, width), BF),
            pltpu.VMEM((max(2, 2 * brow // LANES), 1, LANES), F32),
            pltpu.VMEM((ncl * SLOT, width), BF),
            pltpu.VMEM((ncl, 1, LANES), F32),
            pltpu.VMEM((pages, ncl * SLOT), BF),
            pltpu.VMEM((pages, LANES), jnp.int32),
        ]
        + [dma(ncol)] * 10
        + [dma(4 * ngr)] * 2
        + [dma(ncol)] * 4
        + [dma(7)] * 2
        + [dma(ncl)] * 4,
        compiler_params=pltpu.CompilerParams(
            collective_id=0, has_side_effects=True, vmem_limit_bytes=60 * 2**20
        ),
        name="dedup",
    )(embeddings, cluster.reshape(1, pages), cluster)
    return dup.reshape(pages), near


def solution(mesh):
    ncol = mesh.shape["shard"] // 2
    nx = 1
    while nx * nx < ncol:
        nx *= 2
    return jax.shard_map(
        functools.partial(local, (ncol // nx, nx)),
        mesh=mesh,
        in_specs=(P(("shard", "grp"), None), P(("shard", "grp"), None)),
        out_specs=(P(("shard", "grp")), P(("shard", "grp"), None)),
        check_vma=False,
    )
```

```python
import functools
import math

import jax
import jax.numpy as jnp
from jax import lax
from jax.experimental import pallas as pl
from jax.experimental.pallas import tpu as pltpu
from jax.sharding import PartitionSpec as P

SLOT = 32
LANES = 128
BF = jnp.bfloat16
F32 = jnp.float32
OWN, CROSS, PARTNER, FAR = range(4)
MESH = pl.DeviceIdType.MESH


def offsets(ny, nx):
    def far(o):
        return min(o[0], ny - o[0]) + min(o[1], nx - o[1])

    return sorted(((dy, dx) for dy in range(ny) for dx in range(nx)), key=lambda o: (far(o), o))


def kernel(
    ny, nx, nz,
    emb_hbm, idr, near, dup,
    emb, units, ob, f0, xs, fx, rl, fr, acc, cn, res, dsend, back, drecv, unpack, slot_c, total,
    ems, s1s, s1r, rls, rlr, xrs, xrr, pws, pwr, pfs, pfr, sbs, sbr,
    fos, fors, frs, frr, fbs, fbr, res_s, res_r, dus, dur,
):
    offs = offsets(ny, nx)
    ncol = ny * nx
    ncl = 2 * ncol
    half = ncol // 2
    pages, width = emb.shape
    hrow = half * SLOT
    lw = min(LANES, hrow)
    per = lw // SLOT
    shard, z = lax.axis_index("shard"), lax.axis_index("grp")
    q, core = shard // 2, shard % 2
    y, x = q // nx, q % nx
    side = z // 2

    def column(n, sign):
        dy, dx = offs[n]
        yy = lax.rem(y + (dy if sign > 0 else ny - dy), ny)
        xx = lax.rem(x + (dx if sign > 0 else nx - dx), nx)
        return yy * nx + xx

    def at(col, c, zz):
        return {"shard": col * 2 + c, "grp": zz}

    cross_z = nz - 1 - z
    sibling = at(q, 1 - core, z)
    partner = at(q, core, z + 1 - 2 * (z % 2))
    cross = at(q, core, cross_z)

    def rcopy(src, dst, ss, rs, dev):
        return pltpu.make_async_remote_copy(
            src_ref=src, dst_ref=dst, send_sem=ss, recv_sem=rs, device_id=dev, device_id_type=MESH
        )

    barrier = pltpu.get_barrier_semaphore()
    peers = [at(column(n, 1), core, z) for n in reversed(range(1, ncol))] + [cross, partner, sibling]
    for peer in peers:
        pl.semaphore_signal(barrier, inc=1, device_id=peer, device_id_type=MESH)

    parts = ems.shape[0]
    prow = pages // parts
    loads = [
        pltpu.make_async_copy(
            emb_hbm.at[pl.ds(k * prow, prow), :], emb.at[pl.ds(k * prow, prow), :], ems.at[k]
        )
        for k in range(parts)
    ]
    for c in loads:
        c.start()

    ids = idr[...]
    col, b = ids // 2, ids % 2
    dy = lax.rem(col // nx - y + ny, ny)
    dx = lax.rem(col % nx - x + nx, nx)
    near_rank = jnp.zeros_like(ids)
    for n, o in enumerate(offs):
        near_rank = jnp.where((dy == o[0]) & (dx == o[1]), n, near_rank)
    rid = jnp.where(b == side, 0, ncol) + near_rank
    hot_t = (lax.broadcasted_iota(jnp.int32, (ncl, pages), 0) == rid).astype(BF)
    upto = lax.broadcasted_iota(jnp.int32, (pages, pages), 0)
    upto = (upto <= lax.broadcasted_iota(jnp.int32, (pages, pages), 1)).astype(BF)
    cum_t = jnp.dot(hot_t, upto, preferred_element_type=F32)
    hot_f = hot_t.astype(F32)
    rank = jnp.sum(cum_t * hot_f, axis=0, keepdims=True) - 1.0
    slot = rid * SLOT + rank.astype(jnp.int32)
    held = jnp.sum(hot_f, axis=1, keepdims=True)
    lane = lax.broadcasted_iota(jnp.int32, (ncl, LANES), 1) % SLOT
    flags = (lane.astype(F32) < held).astype(F32)
    for c in range(ncl):
        f0[c] = flags[c : c + 1, :]

    for k, c in enumerate(loads):
        c.wait()
        rows = emb[pl.ds(k * prow, prow), :]
        scale = lax.rsqrt(jnp.mean(rows * rows, axis=1, keepdims=True) + 1e-06)
        units[pl.ds(k * prow, prow), :] = (rows * scale).astype(BF)
    step = ncl * SLOT // 4
    for j in range(4):
        pick = lax.broadcasted_iota(jnp.int32, (step, pages), 0) + j * step == slot
        ob[pl.ds(j * step, step), :] = jnp.dot(
            pick.astype(BF), units[...], preferred_element_type=F32
        ).astype(BF)

    pl.semaphore_wait(barrier, len(peers))

    def chunk(ref, n, count=1):
        return ref.at[pl.ds(n * SLOT, count * SLOT), :]

    def block(role, kap, n, count=1):
        return chunk(xs.at[role, n // half, kap], n % half, count)

    own_in, rel_in, fo_in, fr_in, started = {}, {}, {}, {}, []
    for n in range(ncol):
        oc, rc = chunk(ob, n), chunk(ob, ncol + n)
        if n == 0:
            own_in[n] = pltpu.make_async_copy(oc, block(OWN, 0, 0), s1r.at[0])
            rel_in[n] = pltpu.make_async_copy(rc, chunk(rl, 0), rlr.at[0])
            fo_in[n] = pltpu.make_async_copy(f0.at[0], fx.at[OWN, 0, 0], fors.at[0])
            fr_in[n] = pltpu.make_async_copy(f0.at[ncol], fr.at[0], frr.at[0])
        else:
            dev = at(column(n, 1), core, z)
            own_in[n] = rcopy(oc, block(OWN, 0, n), s1s.at[n], s1r.at[n], dev)
            rel_in[n] = rcopy(rc, chunk(rl, n), rls.at[n], rlr.at[n], dev)
            fo_in[n] = rcopy(f0.at[n], fx.at[OWN, 0, n], fos.at[n], fors.at[n], dev)
            fr_in[n] = rcopy(f0.at[ncol + n], fr.at[n], frs.at[n], frr.at[n], dev)
            started += [own_in[n], rel_in[n], fo_in[n], fr_in[n]]
        for c in (own_in[n], rel_in[n], fo_in[n], fr_in[n]):
            c.start()

    def arrived(c, here=False):
        if here:
            c.wait()
        else:
            c.wait_recv()

    def go(c):
        c.start()
        started.append(c)

    rel_out, own_out, far_out = {}, {}, {}
    for n in range(ncol):
        rel_out[n] = rcopy(chunk(rl, n), block(CROSS, 0, n), xrs.at[n], xrr.at[n], cross)
        own_out[n] = rcopy(block(OWN, 0, n), block(PARTNER, 0, n), pws.at[n], pwr.at[n], partner)
        far_out[n] = rcopy(block(CROSS, 0, n), block(FAR, 0, n), pfs.at[n], pfr.at[n], partner)
    group = min(4, half)
    ngr = ncol // group
    sib = {}
    for r in range(4):
        for g in range(ngr):
            k = r * ngr + g
            sib[r, g] = rcopy(
                block(r, 0, g * group, group), block(r, 1, g * group, group), sbs.at[k], sbr.at[k], sibling
            )
    flag_cross = rcopy(fr, fx.at[CROSS, 0], fbs.at[0], fbr.at[0], cross)
    flag_own = rcopy(fx.at[OWN, 0], fx.at[PARTNER, 0], fbs.at[1], fbr.at[1], partner)
    flag_far = rcopy(fx.at[CROSS, 0], fx.at[FAR, 0], fbs.at[2], fbr.at[2], partner)
    flag_sib = [rcopy(fx.at[r, 0], fx.at[r, 1], fbs.at[3 + r], fbr.at[3 + r], sibling) for r in range(4)]
    inbound = {OWN: own_in, CROSS: rel_out, PARTNER: own_out, FAR: far_out}

    def take(role, n):
        arrived(inbound[role][n], role == OWN and n == 0)
        if role == OWN:
            go(own_out[n])
        if n % group == group - 1:
            go(sib[role, n // group])

    def relay(n):
        arrived(rel_in[n], n == 0)
        go(rel_out[n])

    def flags_first():
        for n in range(ncol):
            arrived(fo_in[n], n == 0)
            arrived(fr_in[n], n == 0)
        go(flag_cross)
        go(flag_own)
        go(flag_sib[OWN])

    def flags_next():
        arrived(flag_cross)
        go(flag_far)
        go(flag_sib[CROSS])
        arrived(flag_own)
        go(flag_sib[PARTNER])
        for r in (OWN, CROSS, PARTNER):
            arrived(flag_sib[r])

    def flags_last():
        arrived(flag_far)
        go(flag_sib[FAR])
        arrived(flag_sib[FAR])

    def plan_unpack():
        wide = jnp.broadcast_to(slot.astype(F32), (LANES, pages)).T.astype(jnp.int32)
        slot_c[...] = wide
        lanes = lax.broadcasted_iota(jnp.int32, (pages, LANES), 1)
        for k in range(ncl * SLOT // LANES):
            unpack[:, k * LANES : (k + 1) * LANES] = (lanes + k * LANES == wide).astype(BF)

    def masks_of(role, h):
        out = []
        which = lax.broadcasted_iota(jnp.int32, (1, LANES), 1) // SLOT
        for kap in range(2):
            for g in range(hrow // lw):
                m = jnp.zeros((1, LANES), F32)
                for k in range(per):
                    m = jnp.where(which == k, fx[role, kap, h * half + g * per + k], m)
                out.append(m[:, :lw])
        return out

    def weigh(rows, cols, masks, diag):
        s = lax.dot_general(rows, cols, (((1,), (1,)), ((), ())), preferred_element_type=F32)
        w = jnp.exp2(s * (64.0 / width * math.log2(math.e)))
        if diag:
            a = lax.broadcasted_iota(jnp.int32, w.shape, 0)
            a = jnp.where(a >= hrow, a + hrow, a)
            w = jnp.where(a == lax.broadcasted_iota(jnp.int32, w.shape, 1), 0.0, w)
        count = sum(w[:, k * lw : (k + 1) * lw] * m for k, m in enumerate(masks))
        return count, jnp.dot(w.astype(BF), cols, preferred_element_type=F32)

    def rows_of(rb):
        return jnp.concatenate([xs[rb, 0, 0], xs[rb, 1, 0]], axis=0)

    def columns(role, halves):
        if len(halves) == 2:
            return xs[role].reshape(4 * hrow, width)
        return xs[role, halves[0]].reshape(2 * hrow, width)

    def compute(rb, role, halves):
        masks = sum((masks_of(role, h) for h in halves), [])
        count, pull = weigh(rows_of(rb), columns(role, halves), masks, rb == role)
        sl = pl.ds(rb * 2 * hrow, 2 * hrow)
        if role == OWN:
            cn[sl, :] = count
            acc[sl, :] = pull
        else:
            cn[sl, :] += count
            acc[sl, :] += pull

    def need_sib(r, halves):
        for g in range(ngr):
            if g * group // half in halves:
                arrived(sib[r, g])

    back_in = {}

    def finish(rb, h):
        t = rb * 2 + h
        sl = pl.ds(t * hrow, hrow)
        count, pull = weigh(xs[rb, h, 0], columns(FAR, (1,)), masks_of(FAR, 1), False)
        count = cn[sl, :] + count
        pull = (acc[sl, :] + pull) / (1.0 + jnp.sum(count, axis=1, keepdims=True))
        res[sl, :] = pull.astype(BF)
        value = jnp.log1p(jnp.sum(count.T, axis=0, keepdims=True))
        for g in range(hrow // lw):
            dsend[t * (hrow // lw) + g, :, pl.ds(0, lw)] = value[:, g * lw : (g + 1) * lw]
        back_in[t] = []
        for k in reversed(range(half)):
            n = h * half + k
            m = rb * ncol + n
            d = dsend.at[m // per]
            if m == 0:
                a = pltpu.make_async_copy(chunk(res, m), chunk(back, m), res_r.at[m])
                e = pltpu.make_async_copy(d, drecv.at[m], dur.at[m])
                a.start()
                e.start()
            else:
                dev = at(column(n, -1), core, z if rb == 0 else cross_z)
                a = rcopy(chunk(res, m), chunk(back, m), res_s.at[m], res_r.at[m], dev)
                e = rcopy(d, drecv.at[m], dus.at[m], dur.at[m], dev)
                go(a)
                go(e)
            back_in[t].append((a, e, m == 0))

    plan_unpack()
    sent = 0
    for n in range(ncol):
        take(OWN, n)
        relay(n)
        if n >= 2:
            take(CROSS, n - 2)
        if n >= 4 and n % 2 == 0:
            go(far_out[sent])
            sent += 1
    flags_first()
    take(CROSS, ncol - 2)
    take(CROSS, ncol - 1)
    flags_next()
    for n in range(sent, ncol):
        go(far_out[n])
    need_sib(OWN, (0, 1))
    compute(0, OWN, (0, 1))
    compute(1, OWN, (0, 1))
    need_sib(CROSS, (0, 1))
    compute(0, CROSS, (0, 1))
    for n in range(ncol):
        take(PARTNER, n)
    compute(1, CROSS, (0, 1))
    need_sib(PARTNER, (0, 1))
    compute(0, PARTNER, (0, 1))
    for n in range(half):
        take(FAR, n)
    compute(1, PARTNER, (0, 1))
    flags_last()
    need_sib(FAR, (0,))
    compute(0, FAR, (0,))
    compute(1, FAR, (0,))
    for n in range(half, ncol):
        take(FAR, n)
    need_sib(FAR, (1,))
    tiles = [(0, 1), (1, 1), (0, 0), (1, 0)]
    for rb, h in tiles:
        finish(rb, h)

    for k, (rb, h) in enumerate(tiles):
        t = rb * 2 + h
        for a, _, here in back_in[t]:
            arrived(a, here)
        part = jnp.dot(
            unpack[:, t * hrow : (t + 1) * hrow], back[t * hrow : (t + 1) * hrow, :],
            preferred_element_type=F32,
        )
        if k == 0:
            total[...] = part
        elif k < 3:
            total[...] += part
        else:
            near[...] = (total[...] + part).astype(BF)
    for t in range(4):
        for _, e, here in back_in[t]:
            arrived(e, here)
    got = jnp.concatenate([drecv[n] for n in range(ncl)], axis=0)
    at_slot = slot_c[...]
    hot = (lax.broadcasted_iota(jnp.int32, (pages, ncl), 1) == at_slot[:, :ncl] // SLOT).astype(BF)
    hi = got.astype(BF)
    mid = (got - hi.astype(F32)).astype(BF)
    lo = (got - hi.astype(F32) - mid.astype(F32)).astype(BF)
    picked = sum(jnp.dot(hot, v, preferred_element_type=F32) for v in (lo, mid, hi))
    here = lax.broadcasted_iota(jnp.int32, (pages, LANES), 1) == at_slot % lw
    dup[...] = jnp.sum(jnp.where(here, picked, 0.0).T, axis=0, keepdims=True)
    for c in started:
        c.wait_send()


def widen(a, d, near, dup):
    near[...] = a[...].astype(F32)
    dup[...] = d[...]


def local(grid, embeddings, cluster):
    pages, width = embeddings.shape
    nz = lax.axis_size("grp")
    ny, nx = grid
    ncol = ny * nx
    ncl = 2 * ncol
    half = ncol // 2
    hrow = half * SLOT
    lw = min(LANES, hrow)
    ngr = ncol // min(4, half)
    dma = lambda n: pltpu.SemaphoreType.DMA((n,))
    vmem = pl.BlockSpec(memory_space=pltpu.VMEM)
    near, dup = pl.pallas_call(
        functools.partial(kernel, ny, nx, nz),
        out_shape=(
            jax.ShapeDtypeStruct((pages, width), BF),
            jax.ShapeDtypeStruct((1, pages), F32),
        ),
        in_specs=[pl.BlockSpec(memory_space=pl.ANY), vmem],
        out_specs=(vmem, vmem),
        scratch_shapes=[
            pltpu.VMEM((pages, width), F32),
            pltpu.VMEM((pages, width), BF),
            pltpu.VMEM((ncl * SLOT, width), BF),
            pltpu.VMEM((ncl, 1, LANES), F32),
            pltpu.VMEM((4, 2, 2, hrow, width), BF),
            pltpu.VMEM((4, 2, ncol, 1, LANES), F32),
            pltpu.VMEM((2 * hrow, width), BF),
            pltpu.VMEM((ncol, 1, LANES), F32),
            pltpu.VMEM((4 * hrow, width), F32),
            pltpu.VMEM((4 * hrow, lw), F32),
            pltpu.VMEM((4 * hrow, width), BF),
            pltpu.VMEM((4 * hrow // lw, 1, LANES), F32),
            pltpu.VMEM((ncl * SLOT, width), BF),
            pltpu.VMEM((ncl, 1, LANES), F32),
            pltpu.VMEM((pages, ncl * SLOT), BF),
            pltpu.VMEM((pages, LANES), jnp.int32),
            pltpu.VMEM((pages, width), F32),
            dma(4),
        ]
        + [dma(ncol)] * 10
        + [dma(4 * ngr)] * 2
        + [dma(ncol)] * 4
        + [dma(7)] * 2
        + [dma(ncl)] * 4,
        compiler_params=pltpu.CompilerParams(
            collective_id=0, has_side_effects=True, vmem_limit_bytes=60 * 2**20
        ),
        name="dedup",
    )(embeddings, cluster.reshape(1, pages))
    grain = pages
    near, dup = pl.pallas_call(
        widen,
        grid=(1,),
        out_shape=(
            jax.ShapeDtypeStruct((pages, width), F32),
            jax.ShapeDtypeStruct((1, pages), F32),
        ),
        in_specs=[
            pl.BlockSpec((grain, width), lambda i: (i, 0)),
            pl.BlockSpec((1, pages), lambda i: (0, 0)),
        ],
        out_specs=(
            pl.BlockSpec((grain, width), lambda i: (i, 0)),
            pl.BlockSpec((1, pages), lambda i: (0, 0)),
        ),
        name="widen",
    )(near, dup)
    return dup.reshape(pages), near


def solution(mesh):
    ncol = mesh.shape["shard"] // 2
    nx = 1
    while nx * nx < ncol:
        nx *= 2
    return jax.shard_map(
        functools.partial(local, (ncol // nx, nx)),
        mesh=mesh,
        in_specs=(P(("shard", "grp"), None), P(("shard", "grp"), None)),
        out_specs=(P(("shard", "grp")), P(("shard", "grp"), None)),
        check_vma=False,
    )
```
